256 devices in a mesh: seq: 64 (over x, z, core), tp: 4 (over y).
Axes of the slice: x: 4, y: 4, z: 8, core: 2. Of those that a mesh axis runs over, the one named last changes fastest.
Arguments:
- queries: bfloat16 [65536, 2048], P('seq', 'tp'), may hold values from -6.5 to 6.5
- db_keys: bfloat16 [1024, 128, 2048], P('seq', None, 'tp'), may hold values from -6 to 6
- db_values: bfloat16 [1024, 128, 2048], P('seq', None, 'tp'), may hold values from -12 to 12
- nb_shard: int32 [1024, 2], P('seq'), may hold values from 0 to 63, all different within a row; in each aligned block of 16 rows (0 to 15, 16 to 31, ...) at most 2 rows name the same one
- nb_row: int32 [1024, 2], P('seq'), may hold values from 0 to 15
- out_weight: bfloat16 [2048, 4096], P('seq', 'tp'), may hold values from -0.125 to 0.125
Outputs:
- mixed: bfloat16 [65536, 4096], P('seq', 'tp')
The draws below stay inside these ranges and needn't reach their ends.
Inputs may be any that keep to these rules, and one draw needn't show every extreme that they name: `nb_shard`: among the 16 blocks of one index of seq no shard is named more than 2 times, a bound that some block reaches in some such group; the 2 shards of one block differ.
All inputs are finite; a program needn't handle non-finite values.
Results may differ from the reference program's by a relative error of at most 0.024.
Values may be sent and summed in bfloat16 or wider, within the bound.
No kernel may reach another device: no remote copies, remote signals or barrier semaphores. Data moves between devices by JAX's collectives and lax.ppermute only.
A program may use at most 192 MiB of HBM per device.

```python
import math
import jax
import jax.numpy as jnp
import numpy as np
from jax import lax

D = 4096
HD = 128
BLOCK = 64
NBR = 2
NLEN = 128
TOK_DEV = 1024
DB_DEV = 16
HQ = 2048
BLOCKS_DEV = 16
CAP = 2
TOKENS = 65536
NBLOCKS = 1024
DB_ROWS = 1024
N_SEQ = 64
N_TP = 4


def draw_queries(key, part):
    drawn = jnp.clip(jax.random.normal(jax.random.fold_in(key, 11), (TOKENS, HQ), jnp.float32), -4.0, 4.0)
    return drawn.astype(jnp.bfloat16)


def draw_db_keys(key, part):
    drawn = 1.5 * jnp.clip(jax.random.normal(jax.random.fold_in(key, 23), (DB_ROWS, NLEN, HQ), jnp.float32), -4.0, 4.0)
    return drawn.astype(jnp.bfloat16)


def with_ends(result, stream_key, smallest, top_value):
    dims = result.shape
    index_at = [jax.random.randint(jax.random.fold_in(stream_key, axis), (), 0, dims[axis]) for axis in range(len(dims))]
    result = result.at[tuple(index_at)].set(smallest)
    longest = dims.index(max(dims))
    index_at[longest] = (index_at[longest] + 1) % dims[longest]
    return result.at[tuple(index_at)].set(top_value)


def levels(rng, shape, cuts, smallest, high):
    loudness, own = 1.0, jax.random.fold_in(rng, 6)
    for position, blocks in cuts:
        draws = jnp.exp(jax.random.uniform(jax.random.fold_in(own, position), (blocks,), jnp.float32, smallest / len(cuts), high / len(cuts)))
        loudness = loudness * jnp.repeat(draws, shape[position] // blocks).reshape([-1 if axis == position else 1 for axis in range(len(shape))])
    return loudness


def cumulative_ranks(number_of, skew):
    portions = [(1 << 20) // math.isqrt(standing ** skew) + 1 for standing in range(1, number_of + 1)]
    width = 1 + sum(portions) // (1 << 30)
    return np.cumsum(np.array([max(1, weight // width) for weight in portions]))


def ranked_ids(rng, dims, number_of, lean):
    listing = cumulative_ranks(number_of, lean)
    lot = jax.random.randint(jax.random.fold_in(rng, 1), dims, 0, int(listing[number_of - 1]))
    rank = jnp.searchsorted(jnp.asarray(listing, jnp.int32), lot, side="right")
    return jax.random.permutation(jax.random.fold_in(rng, 2), number_of)[rank].astype(jnp.int32)


def deal_out(own_key, own, number, rows, number_of, top, bound, lean):
    order = jax.random.permutation(own_key, number_of)
    packed, usual = load_shares(number_of, rows * top, bound, lean, True), load_shares(number_of, rows * top, bound, lean, False)
    places = jnp.arange(number_of)

    def named(lengths, offset_by):
        used = int((lengths > 0).sum())
        fixed = max(1, used // 4)
        moved = fixed + (places - fixed + offset_by * (used - fixed)) % max(1, number_of - fixed)
        return jnp.zeros((number_of,), jnp.int32).at[order[jnp.where(places < fixed, places, moved)]].set(jnp.asarray(lengths, jnp.int32))

    lengths = jnp.where(number % 4 == 0, named(packed, number // 4), named(usual, number - number // 4 - 1))
    mixed = jax.random.permutation(jax.random.fold_in(own, 3), number_of)
    giver, sink = mixed[0:number_of // 2 * 2:2], mixed[1:number_of // 2 * 2:2]
    room = jnp.minimum(lengths[giver] - 1, bound - lengths[sink]) // 2
    room = jnp.where((giver == order[0]) | (sink == order[0]) | (lengths[sink] == 0), 0, jnp.maximum(room, 0))
    moved = jax.random.randint(jax.random.fold_in(own, 4), (number_of // 2,), 0, 1 << 20) % (room + 1)
    lengths = lengths.at[giver].add(-moved).at[sink].add(moved)
    items = jnp.searchsorted(jnp.cumsum(lengths), jnp.arange(rows * top), side="right").astype(jnp.int32)
    listing = items.reshape(top, rows).T
    listing = listing[jax.random.permutation(jax.random.fold_in(own, 1), rows)]
    offset_by = jax.random.randint(jax.random.fold_in(own, 2), (rows, 1), 0, top)
    return jnp.take_along_axis(listing, (jnp.arange(top)[None, :] + offset_by) % top, axis=1)


def load_shares(count, total, limit, lean, full):
    portions = [(1 << 20) // math.isqrt(grade ** lean) + 1 for grade in range(1, count + 1)]
    largest = limit if full else min(limit, max(-(-total // count), total * portions[0] // sum(portions)))
    least = 1 if total - largest >= count - 1 else 0
    counts, surplus = [largest] + [least] * (count - 1), total - largest - least * (count - 1)
    while surplus > 0:
        movable = [i for i in range(1, count) if counts[i] < largest] or [i for i in range(1, count) if counts[i] < limit]
        whole, remaining = sum([portions[i] for i in movable]), surplus
        for i in movable:
            addition = min(limit - counts[i], max(1, remaining * portions[i] // whole), surplus)
            counts[i] = counts[i] + addition
            surplus = surplus - addition
    return np.array(counts)


def noise(own_key, extent, deviation, bound, cuts=(), held_as=jnp.bfloat16):
    values = deviation * jax.random.normal(own_key, extent, jnp.float32)
    if cuts:
        values = values * levels(own_key, extent, cuts, -0.22, 0.18)
    return jnp.clip(values, -bound, bound).astype(held_as)


def setup_inputs(seed: int = 0) -> dict:
    arg_keys = jax.random.split(jax.random.key(seed), 7)
    queries = draw_queries(jax.random.fold_in(arg_keys[6], 71), 0)
    db_keys = draw_db_keys(jax.random.fold_in(arg_keys[6], 71), 0)
    db_values = noise(arg_keys[2], (DB_ROWS, NLEN, HQ), 3.0, 12.0, ((0, 64), (2, 4)))
    nb_shard_keys = jax.random.split(jax.random.fold_in(arg_keys[3], 1), NBLOCKS // BLOCKS_DEV)
    nb_shard_turns = jax.random.permutation(jax.random.fold_in(arg_keys[3], 3), NBLOCKS // BLOCKS_DEV)
    nb_shard = jax.vmap(lambda own, number: deal_out(jax.random.fold_in(arg_keys[3], 2), own, number, BLOCKS_DEV, N_SEQ, NBR, CAP, 2))(nb_shard_keys, nb_shard_turns).reshape((NBLOCKS, NBR))
    nb_row = with_ends(ranked_ids(arg_keys[4], (NBLOCKS, NBR), DB_DEV, 2), jax.random.fold_in(arg_keys[4], 3), 0, DB_DEV - 1).astype(jnp.int32)
    out_weight = noise(arg_keys[5], (HQ, D), HQ ** -0.5, 0.125, ((0, 64), (1, 4)))
    return dict(queries=queries, db_keys=db_keys, db_values=db_values, nb_shard=nb_shard, nb_row=nb_row, out_weight=out_weight)


def reference(queries, db_keys, db_values, nb_shard, nb_row, out_weight):
    score_scale = float(HD) ** -0.5
    tokens = queries.shape[0]
    feature_cols = queries.shape[1]
    heads_all = feature_cols // HD
    shifted = jnp.concatenate([queries[BLOCK - 1:], jnp.zeros((BLOCK - 1, feature_cols), queries.dtype)], axis=0)
    shifted = shifted.reshape(N_SEQ, BLOCKS_DEV, BLOCK, heads_all, HD)
    entry_index = (nb_shard * DB_DEV + nb_row).astype(jnp.int32).reshape(N_SEQ, BLOCKS_DEV, NBR)

    def attend_block(block_args):
        query_block, index_block = block_args
        key_rows = db_keys[index_block].astype(jnp.float32).reshape(BLOCKS_DEV, NBR, NLEN, heads_all, HD)
        value_rows = db_values[index_block].astype(jnp.float32).reshape(BLOCKS_DEV, NBR, NLEN, heads_all, HD)
        scores = jnp.einsum("bqhd,bnkhd->bnhqk", query_block.astype(jnp.float32), key_rows) * score_scale
        row_max = jnp.max(scores, axis=-1, keepdims=True)
        log_total = row_max[..., 0] + jnp.log(jnp.sum(jnp.exp(scores - row_max), axis=-1))
        weights = jnp.exp(scores - log_total[..., None]).astype(jnp.bfloat16)
        partial_value = jnp.einsum("bnhqk,bnkhd->bnqhd", weights.astype(jnp.float32), value_rows).astype(jnp.bfloat16)
        best_log = jnp.max(log_total, axis=1, keepdims=True)
        merged_log = best_log + jnp.log(jnp.sum(jnp.exp(log_total - best_log), axis=1, keepdims=True))
        share = jnp.transpose(jnp.exp(log_total - merged_log), (0, 1, 3, 2))[..., None]
        attended = jnp.sum(share * partial_value.astype(jnp.float32), axis=1).astype(jnp.bfloat16)
        return attended.reshape(BLOCKS_DEV * BLOCK, feature_cols)

    attended = lax.map(attend_block, (shifted, entry_index)).reshape(tokens, feature_cols)
    placed = jnp.concatenate([jnp.zeros((BLOCK - 1, feature_cols), jnp.bfloat16), attended[:tokens - (BLOCK - 1)]], axis=0)
    group_cols = feature_cols // N_TP

    def project_rows(row_block):
        summed = jnp.zeros((row_block.shape[0], out_weight.shape[1]), jnp.float32)
        for group in range(N_TP):
            product = jnp.dot(row_block[:, group * group_cols:(group + 1) * group_cols], out_weight[group * group_cols:(group + 1) * group_cols], preferred_element_type=jnp.float32)
            rounded = lax.optimization_barrier(product.astype(jnp.bfloat16))
            summed = summed + rounded.astype(jnp.float32)
        return summed.astype(jnp.bfloat16)

    mixed = lax.map(project_rows, placed.reshape(N_SEQ, TOK_DEV, feature_cols))
    return mixed.reshape(tokens, out_weight.shape[1])
```

```python
import functools

import jax
import jax.numpy as jnp
from jax import lax
from jax.experimental import pallas as pl
from jax.experimental.pallas import tpu as pltpu
from jax.sharding import Mesh, PartitionSpec as P

HD = 128
BLOCK = 64
NBR = 2
NLEN = 128
NX, NZ, NC, NT = 4, 8, 2, 4
BLOCKS = 16
ROWS = BLOCKS * BLOCK
HEADS = 2
COLS = HEADS * HD
LROWS = BLOCKS
MSG = ROWS + LROWS
HALF = ROWS // 2
SRC = (4, 3, -3, 2, -2, 1, -1, 0)
MAXREQ = 128
BATCH = 4
EMPTY = -1e30
NOTHING = -2e30
VMEM_LIMIT = 60 * 1024 * 1024


def shift(value, axis, by):
    count = lax.axis_size(axis)
    return lax.ppermute(value, axis, [(i, (i - by) % count) for i in range(count)])


def seq_shift(value, by):
    count = NX * NZ * NC
    pairs = [(i, i - by) for i in range(count) if 0 <= i - by < count]
    return lax.ppermute(value, ("x", "z", "c"), pairs)


def attend_kernel(count_ref, where_ref, entry_ref, *refs):
    n_q = 9
    q_refs = refs[:n_q]
    kv0, kv0c, kv1, kv1c, kv3, kv3c, k2, k2c, v2, v2c = refs[n_q : n_q + 10]
    first_ref, out_ref, qs, kvs, lts, sems = refs[n_q + 10 :]
    col = first_ref[0]
    copies = []

    def put(src, dst):
        copy = pltpu.make_async_copy(src, dst, sems.at[len(copies)])
        copy.start()
        copies.append(copy)

    for s, q in enumerate(q_refs):
        if s < 2:
            put(q.at[:, pl.ds(col, COLS)], qs.at[0, pl.ds(s * HALF, HALF)])
        else:
            put(q.at[:, pl.ds(col, COLS)], qs.at[s - 1])
    for j, ref in ((0, kv0), (1, kv0c), (2, kv1), (3, kv1c), (6, kv3), (7, kv3c)):
        put(ref, kvs.at[:, pl.ds(j * 16, 16)])
    for j, ref in ((4, k2), (5, k2c)):
        put(ref, kvs.at[0, pl.ds(j * 16, 16)])
    for j, ref in ((4, v2), (5, v2c)):
        put(ref, kvs.at[1, pl.ds(j * 16, 16)])
    lts[...] = jnp.full(lts.shape, EMPTY, jnp.float32)
    for s in range(len(SRC)):
        out_ref[s, 0:ROWS, :] = jnp.zeros((ROWS, COLS), jnp.bfloat16)
    for copy in copies:
        copy.wait()
    total = count_ref[0]
    lane = lax.broadcasted_iota(jnp.int32, (BLOCK, 128), 1)
    scale = float(HD) ** (-0.5)

    def batch(step, carry):
        found = []
        for i in range(BATCH):
            r = step * BATCH + i
            place = where_ref[r]
            entry = entry_ref[r]
            s = place // BLOCKS
            b = place % BLOCKS
            rows = pl.ds(pl.multiple_of(b * BLOCK, BLOCK), BLOCK)
            for h in range(HEADS):
                cols = slice(h * HD, (h + 1) * HD)
                scores = (
                    lax.dot_general(
                        qs[s, rows, cols],
                        kvs[0, entry, :, cols],
                        (((1,), (1,)), ((), ())),
                        preferred_element_type=jnp.float32,
                    )
                    * scale
                )
                top = jnp.max(scores, axis=-1, keepdims=True)
                weights = jnp.exp(scores - top)
                total_w = jnp.sum(weights, axis=-1, keepdims=True)
                value = jnp.dot(
                    weights.astype(jnp.bfloat16),
                    kvs[1, entry, :, cols],
                    preferred_element_type=jnp.float32,
                )
                logs = jnp.where(r < total, top + jnp.log(total_w), NOTHING)
                found.append((s, b, rows, h, cols, logs, value / total_w))
        for s, b, rows, h, cols, logs, value in found:
            held_logs = lts[s, h * BLOCK : (h + 1) * BLOCK, :]
            here = lane == b
            old = jnp.sum(jnp.where(here, held_logs, 0.0), axis=-1, keepdims=True)
            best = jnp.maximum(old, logs)
            keep = jnp.exp(old - best)
            add = jnp.exp(logs - best)
            both = keep + add
            lts[s, h * BLOCK : (h + 1) * BLOCK, :] = jnp.where(
                here, best + jnp.log(both), held_logs
            )
            held = out_ref[s, rows, cols].astype(jnp.float32)
            out_ref[s, rows, cols] = ((keep / both) * held + (add / both) * value).astype(
                jnp.bfloat16
            )
        return carry

    lax.fori_loop(0, (total + BATCH - 1) // BATCH, batch, 0)
    for s in range(len(SRC)):
        store_logs(out_ref.at[s], ROWS, jnp.transpose(lts[s])[0:BLOCKS, :])


def store_logs(ref, base, logs):
    high = logs.astype(jnp.bfloat16)
    ref[base : base + LROWS, 0 : HEADS * BLOCK] = high
    ref[base : base + LROWS, HEADS * BLOCK : 2 * HEADS * BLOCK] = (
        logs - high.astype(jnp.float32)
    ).astype(jnp.bfloat16)


def load_logs(ref, base):
    return ref[base : base + LROWS, 0 : HEADS * BLOCK].astype(jnp.float32) + ref[
        base : base + LROWS, HEADS * BLOCK : 2 * HEADS * BLOCK
    ].astype(jnp.float32)


def shares(logs):
    best = functools.reduce(jnp.maximum, logs)
    terms = [jnp.exp(l - best) for l in logs]
    total = functools.reduce(lambda a, b: a + b, terms)
    return best + jnp.log(total), [t / total for t in terms]


def columns(parts):
    rows = [*parts, jnp.zeros((128 - LROWS * len(parts), 128), jnp.float32)]
    return jnp.transpose(jnp.concatenate(rows, axis=0))


def blend(out, turned, first, block, sources):
    for h in range(HEADS):
        total = None
        for k, (ref, row) in enumerate(sources):
            at = (first + k) * LROWS + block
            share = turned[h * BLOCK : (h + 1) * BLOCK, at : at + 1]
            term = share * ref[row : row + BLOCK, h * HD : (h + 1) * HD].astype(jnp.float32)
            total = term if total is None else total + term
        out[block * BLOCK : (block + 1) * BLOCK, h * HD : (h + 1) * HD] = total.astype(
            jnp.bfloat16
        )


def merge_kernel(halves, own_a, own_b, in_a, in_b, out_a, out_b):
    base = HALF if halves else ROWS
    blocks = BLOCKS // 2 if halves else BLOCKS
    parts = []
    for own, came in ((own_a, in_a), (own_b, in_b)):
        own = own.at[0]
        merged, split = shares([load_logs(own, ROWS), load_logs(came, base)])
        if halves:
            lower = lax.broadcasted_iota(jnp.int32, merged.shape, 0) < blocks
            came_here = lower if came is in_a else jnp.logical_not(lower)
            merged = jnp.where(came_here, merged, load_logs(own, ROWS))
        store_logs(out_a if came is in_a else out_b, ROWS, merged)
        parts += split
    turned = columns(parts)
    for k, (own, came, out) in enumerate(((own_a, in_a, out_a), (own_b, in_b, out_b))):
        own = own.at[0]
        skip = blocks if (halves and k == 1) else 0
        for block in range(BLOCKS):
            rows = slice(block * BLOCK, (block + 1) * BLOCK)
            if skip <= block < skip + blocks:
                blend(
                    out,
                    turned,
                    2 * k,
                    block,
                    [(own, block * BLOCK), (came, (block - skip) * BLOCK)],
                )
            else:
                out[rows, :] = own[rows, :]


def finish_kernel(own, in_a, in_b, out):
    own = own.at[0]
    _, split = shares([load_logs(own, ROWS), load_logs(in_a, ROWS), load_logs(in_b, ROWS)])
    turned = columns(split)
    for block in range(BLOCKS):
        row = block * BLOCK
        blend(out, turned, 0, block, [(own, row), (in_a, row), (in_b, row)])


def whole(shape):
    return pl.BlockSpec(shape, lambda i: (0,) * len(shape))


def own_of(index):
    return pl.BlockSpec((1, MSG, COLS), lambda i: (index, 0, 0))


def params():
    return pltpu.CompilerParams(vmem_limit_bytes=VMEM_LIMIT)


def merge(own, index_a, index_b, in_a, in_b):
    halves = in_a.shape[0] != MSG
    message = jax.ShapeDtypeStruct((MSG, COLS), jnp.bfloat16)
    return pl.pallas_call(
        functools.partial(merge_kernel, halves),
        out_shape=(message, message),
        grid=(1,),
        in_specs=[own_of(index_a), own_of(index_b), whole(in_a.shape), whole(in_b.shape)],
        out_specs=(whole((MSG, COLS)), whole((MSG, COLS))),
        compiler_params=params(),
        cost_estimate=pl.CostEstimate(
            flops=8 * ROWS * COLS, transcendentals=0, bytes_accessed=12 * ROWS * COLS
        ),
        name="merge",
    )(own, own, in_a, in_b)


def finish(own, in_a, in_b):
    return pl.pallas_call(
        finish_kernel,
        out_shape=jax.ShapeDtypeStruct((ROWS, COLS), jnp.bfloat16),
        grid=(1,),
        in_specs=[own_of(len(SRC) - 1), whole((MSG, COLS)), whole((MSG, COLS))],
        out_specs=whole((ROWS, COLS)),
        compiler_params=params(),
        cost_estimate=pl.CostEstimate(
            flops=8 * ROWS * COLS, transcendentals=0, bytes_accessed=8 * ROWS * COLS
        ),
        name="finish",
    )(own, in_a, in_b)


def attend(piece, requests, query_parts, pair_parts):
    count, where, entry = requests
    anywhere = pl.BlockSpec(memory_space=pl.ANY)
    first = jnp.full((1,), piece * COLS, jnp.int32)
    smem = pl.BlockSpec(memory_space=pltpu.SMEM)
    n_in = len(query_parts) + len(pair_parts)

    def kernel(count_ref, where_ref, entry_ref, first_ref, *refs):
        attend_kernel(
            count_ref,
            where_ref,
            entry_ref,
            *refs[:n_in],
            [piece * COLS],
            *refs[n_in:],
        )

    return pl.pallas_call(
        kernel,
        out_shape=jax.ShapeDtypeStruct((len(SRC), MSG, COLS), jnp.bfloat16),
        in_specs=[smem] * 4 + [anywhere] * n_in,
        out_specs=pl.BlockSpec(memory_space=pltpu.VMEM),
        scratch_shapes=[
            pltpu.VMEM((len(SRC), ROWS, COLS), jnp.bfloat16),
            pltpu.VMEM((2, 128, NLEN, COLS), jnp.bfloat16),
            pltpu.VMEM((len(SRC), HEADS * BLOCK, 128), jnp.float32),
            pltpu.SemaphoreType.DMA((n_in,)),
        ],
        compiler_params=params(),
        cost_estimate=pl.CostEstimate(
            flops=MAXREQ * HEADS * 4 * BLOCK * NLEN * HD,
            transcendentals=MAXREQ * HEADS * BLOCK * NLEN,
            bytes_accessed=26 * 1024 * 1024,
        ),
        name="attend",
    )(count, where, entry, first, *query_parts, *pair_parts)


def project_kernel(turn_ref, *refs):
    lhs_refs, w_ref, out_ref, rows = refs[:8], refs[8], refs[9], refs[10]
    for dt in range(NT):
        at = lax.rem(turn_ref[0] + dt, NT) * (2 * COLS)
        for piece in range(2):
            rows[:, pl.ds(pl.multiple_of(at + piece * COLS, COLS), COLS)] = lhs_refs[
                piece * NT + dt
            ][...]
    out_ref[...] = jnp.dot(rows[...], w_ref[...], preferred_element_type=jnp.float32).astype(
        jnp.bfloat16
    )


def project(turn, lhs, weight):
    tile = 256
    depth, width = weight.shape
    return pl.pallas_call(
        project_kernel,
        out_shape=jax.ShapeDtypeStruct((ROWS, width), jnp.bfloat16),
        grid=(ROWS // tile,),
        in_specs=[pl.BlockSpec(memory_space=pltpu.SMEM)]
        + [pl.BlockSpec((tile, COLS), lambda i: (i, 0))] * 8
        + [pl.BlockSpec((depth, width), lambda i: (0, 0))],
        out_specs=pl.BlockSpec((tile, width), lambda i: (i, 0)),
        scratch_shapes=[pltpu.VMEM((tile, depth), jnp.bfloat16)],
        compiler_params=params(),
        cost_estimate=pl.CostEstimate(
            flops=2 * ROWS * depth * width,
            transcendentals=0,
            bytes_accessed=2 * (ROWS * depth + depth * width + ROWS * width),
        ),
        name="project",
    )(turn, *lhs, weight)


def request_list(nb_shard, nb_row):
    my_x, my_z, my_c = (lax.axis_index(a) for a in ("x", "z", "c"))
    table = jnp.stack([nb_shard, nb_row]).reshape(1, 2 * BLOCKS * NBR)
    tables = lax.all_to_all(
        jnp.broadcast_to(table, (NZ, 2 * BLOCKS * NBR)), "z", split_axis=0, concat_axis=0, tiled=True
    )
    order = (my_z + jnp.array(SRC, jnp.int32)) % NZ
    pick = (order[:, None] == jnp.arange(NZ, dtype=jnp.int32)[None, :]).astype(jnp.int32)
    tables = jnp.sum(pick[:, :, None] * tables[None], axis=1)
    shard = tables[:, : BLOCKS * NBR].reshape(-1)
    row = tables[:, BLOCKS * NBR :].reshape(-1)
    valid = (shard // NC) % NZ == my_z
    near = (shard // (NC * NZ) - my_x) % NX
    other = (shard % NC + my_c) % NC
    entry = (near * NC + other) * 16 + row
    where = jnp.arange(shard.shape[0], dtype=jnp.int32) // NBR
    seen = valid.astype(jnp.int32)
    ids = jnp.arange(shard.shape[0], dtype=jnp.int32)
    rank = jnp.sum(jnp.where(ids[None, :] < ids[:, None], seen[None, :], 0), axis=1)
    slot = jnp.arange(MAXREQ, dtype=jnp.int32)
    hit = valid[None, :] & (rank[None, :] == slot[:, None])
    where_list = jnp.sum(jnp.where(hit, where[None, :], 0), axis=1)
    entry_list = jnp.sum(jnp.where(hit, entry[None, :], 0), axis=1)
    return jnp.sum(seen).reshape(1), where_list, entry_list


def per_device(queries, db_keys, db_values, nb_shard, nb_row, out_weight):
    weight = lax.all_gather(out_weight, ("x", "z", "c"), axis=0, tiled=True)
    requests = request_list(nb_shard, nb_row)

    upcoming = seq_shift(queries[:BLOCK], 1)
    extended = jnp.concatenate([queries[BLOCK - 1 :], upcoming[: BLOCK - 1]], axis=0)

    pairs = []
    for piece in range(2):
        cols = slice(piece * COLS, (piece + 1) * COLS)
        own = jnp.stack([db_keys[:, :, cols], db_values[:, :, cols]])
        ahead = shift(own, "x", 1)
        behind = shift(own, "x", -1)
        keys2 = shift(ahead[0], "x", 1)
        values2 = shift(behind[1], "x", -1)
        parts = []
        for part in (own, ahead, behind, keys2, values2):
            parts += [part, shift(part, "c", 1)]
        pairs.append(parts)

    up, down = [extended], [extended]
    for _ in range(3):
        up.append(shift(up[-1], "z", 1))
        down.append(shift(down[-1], "z", -1))
    far_low = shift(up[3][:HALF], "z", 1)
    far_high = shift(down[3][HALF:], "z", -1)
    query_parts = [far_low, far_high, up[3], down[3], up[2], down[2], up[1], down[1], extended]

    gathered = []
    for piece in range(2):
        own = attend(piece, requests, query_parts, pairs[piece])
        far_logs = own[0, ROWS:]
        in_a = shift(jnp.concatenate([own[0, :HALF], far_logs], axis=0), "z", -1)
        in_b = shift(jnp.concatenate([own[0, HALF:ROWS], far_logs], axis=0), "z", 1)
        for step in range(3):
            out_a, out_b = merge(own, 1 + 2 * step, 2 + 2 * step, in_a, in_b)
            in_a = shift(out_a, "z", -1)
            in_b = shift(out_b, "z", 1)
        attended = finish(own, in_a, in_b)
        tail = seq_shift(attended[ROWS - BLOCK :], -1)
        placed = jnp.concatenate([tail[1:], attended[: ROWS - (BLOCK - 1)]], axis=0)
        ahead = shift(placed, "tp", 1)
        behind = shift(placed, "tp", -1)
        low = shift(ahead[:HALF], "tp", 1)
        high = shift(behind[HALF:], "tp", -1)
        gathered += [placed, ahead, jnp.concatenate([low, high], axis=0), behind]
    turn = lax.axis_index("tp").astype(jnp.int32).reshape(1)
    return project(turn, gathered, weight)


def solution(mesh):
    grid = Mesh(mesh.devices.reshape(NX, NZ, NC, NT), ("x", "z", "c", "tp"))
    seq = ("x", "z", "c")
    placed = (
        P(seq, "tp"),
        P(seq, None, "tp"),
        P(seq, None, "tp"),
        P(seq, None),
        P(seq, None),
        P(seq, "tp"),
    )
    return jax.shard_map(
        per_device, mesh=grid, in_specs=placed, out_specs=P(seq, "tp"), check_vma=False
    )
```

```python
import functools

import jax
import jax.numpy as jnp
from jax import lax
from jax.experimental import pallas as pl
from jax.experimental.pallas import tpu as pltpu
from jax.sharding import Mesh, PartitionSpec as P

HD = 128
BLOCK = 64
NBR = 2
NLEN = 128
NX, NZ, NC, NT = 4, 8, 2, 4
BLOCKS = 16
ROWS = BLOCKS * BLOCK
HEADS = 2
COLS = HEADS * HD
LROWS = BLOCKS
MSG = ROWS + LROWS
HALF = ROWS // 2
SRC = (4, 3, -3, 2, -2, 1, -1, 0)
MAXREQ = 128
PLACES = len(SRC) * BLOCKS
BATCH = 4
EMPTY = -1e30
NOTHING = -2e30
VMEM_LIMIT = 60 * 1024 * 1024


def shift(value, axis, by):
    count = lax.axis_size(axis)
    return lax.ppermute(value, axis, [(i, (i - by) % count) for i in range(count)])


def seq_shift(value, by):
    count = NX * NZ * NC
    pairs = [(i, i - by) for i in range(count) if 0 <= i - by < count]
    return lax.ppermute(value, ("x", "z", "c"), pairs)


def after(value, *earlier):
    return lax.optimization_barrier((value, *earlier))[0]


def attend_kernel(count_ref, where_ref, entry_ref, *refs):
    n_q = 9
    q_refs = refs[:n_q]
    kv0, kv0c, kv1, kv1c, kv3, kv3c, k2, k2c, v2, v2c = refs[n_q : n_q + 10]
    first_ref, out_ref, qs, kvs, lts, sems = refs[n_q + 10 :]
    col = first_ref[0]
    copies = []

    def put(src, dst):
        copy = pltpu.make_async_copy(src, dst, sems.at[len(copies)])
        copy.start()
        copies.append(copy)

    for s, q in enumerate(q_refs):
        if s < 2:
            put(q.at[:, pl.ds(col, COLS)], qs.at[0, pl.ds(s * HALF, HALF)])
        else:
            put(q.at[:, pl.ds(col, COLS)], qs.at[s - 1])
    for j, ref in ((0, kv0), (1, kv0c), (2, kv1), (3, kv1c), (6, kv3), (7, kv3c)):
        put(ref, kvs.at[:, pl.ds(j * 16, 16)])
    for j, ref in ((4, k2), (5, k2c)):
        put(ref, kvs.at[0, pl.ds(j * 16, 16)])
    for j, ref in ((4, v2), (5, v2c)):
        put(ref, kvs.at[1, pl.ds(j * 16, 16)])

    def clear(place, carry):
        lts[place] = jnp.full((HEADS * BLOCK, 128), EMPTY, jnp.float32)
        rows = pl.ds(pl.multiple_of((place % BLOCKS) * BLOCK, BLOCK), BLOCK)
        out_ref[place // BLOCKS, rows, :] = jnp.zeros((BLOCK, COLS), jnp.bfloat16)
        return carry

    lax.fori_loop(0, PLACES + 1, clear, 0)
    for copy in copies:
        copy.wait()
    total = count_ref[0]
    scale = float(HD) ** (-0.5)

    def batch(step, carry):
        found = []
        for i in range(BATCH):
            r = step * BATCH + i
            place = where_ref[r]
            entry = entry_ref[r]
            s = place // BLOCKS
            rows = pl.ds(pl.multiple_of((place % BLOCKS) * BLOCK, BLOCK), BLOCK)
            item = []
            for h in range(HEADS):
                cols = slice(h * HD, (h + 1) * HD)
                scores = (
                    lax.dot_general(
                        qs[s % len(SRC), rows, cols],
                        kvs[0, entry, :, cols],
                        (((1,), (1,)), ((), ())),
                        preferred_element_type=jnp.float32,
                    )
                    * scale
                )
                top = jnp.max(scores, axis=-1, keepdims=True)
                weights = jnp.exp(scores - top)
                total_w = jnp.sum(weights, axis=-1, keepdims=True)
                value = jnp.dot(
                    weights.astype(jnp.bfloat16),
                    kvs[1, entry, :, cols],
                    preferred_element_type=jnp.float32,
                )
                logs = jnp.broadcast_to(top + jnp.log(total_w), (BLOCK, 128))
                item.append((logs, value / total_w))
            found.append((place, s, rows, item))
        merged = []
        for i, (place, s, rows, item) in enumerate(found):
            for h in range(HEADS):
                cols = slice(h * HD, (h + 1) * HD)
                at = slice(h * BLOCK, (h + 1) * BLOCK)
                logs = [lts[place, at, :], item[h][0]]
                values = [out_ref[s, rows, cols].astype(jnp.float32), item[h][1]]
                if i:
                    before, _, _, last = found[i - 1]
                    logs.append(jnp.where(before == place, last[h][0], NOTHING))
                    values.append(last[h][1])
                log_total, split = shares(logs)
                value = functools.reduce(
                    lambda a, b: a + b, [w * v for w, v in zip(split, values)]
                )
                merged.append((place, at, s, rows, cols, log_total, value))
        for place, at, s, rows, cols, log_total, value in merged:
            lts[place, at, :] = log_total
            out_ref[s, rows, cols] = value.astype(jnp.bfloat16)
        return carry

    lax.fori_loop(0, (total + BATCH - 1) // BATCH, batch, 0)
    lane = lax.broadcasted_iota(jnp.int32, (HEADS * BLOCK, 128), 1)

    def gather_logs(s, carry):
        logs = jnp.full((HEADS * BLOCK, 128), EMPTY, jnp.float32)
        for b in range(BLOCKS):
            logs = jnp.where(lane == b, lts[s * BLOCKS + b], logs)
        store_logs(out_ref.at[s], ROWS, jnp.transpose(logs)[0:BLOCKS, :])
        return carry

    lax.fori_loop(0, len(SRC), gather_logs, 0)


def store_logs(ref, base, logs):
    high = logs.astype(jnp.bfloat16)
    ref[base : base + LROWS, 0 : HEADS * BLOCK] = high
    ref[base : base + LROWS, HEADS * BLOCK : 2 * HEADS * BLOCK] = (
        logs - high.astype(jnp.float32)
    ).astype(jnp.bfloat16)


def load_logs(ref, base):
    return ref[base : base + LROWS, 0 : HEADS * BLOCK].astype(jnp.float32) + ref[
        base : base + LROWS, HEADS * BLOCK : 2 * HEADS * BLOCK
    ].astype(jnp.float32)


def shares(logs):
    best = functools.reduce(jnp.maximum, logs)
    terms = [jnp.exp(l - best) for l in logs]
    total = functools.reduce(lambda a, b: a + b, terms)
    return best + jnp.log(total), [t / total for t in terms]


def columns(parts):
    rows = [*parts, jnp.zeros((128 - LROWS * len(parts), 128), jnp.float32)]
    return jnp.transpose(jnp.concatenate(rows, axis=0))


def blend(out, turned, first, block, sources):
    for h in range(HEADS):
        total = None
        for k, (ref, row) in enumerate(sources):
            at = (first + k) * LROWS + block
            share = turned[h * BLOCK : (h + 1) * BLOCK, at : at + 1]
            term = share * ref[row : row + BLOCK, h * HD : (h + 1) * HD].astype(jnp.float32)
            total = term if total is None else total + term
        out[block * BLOCK : (block + 1) * BLOCK, h * HD : (h + 1) * HD] = total.astype(
            jnp.bfloat16
        )


def merge_kernel(halves, own_a, own_b, in_a, in_b, out_a, out_b):
    base = HALF if halves else ROWS
    blocks = BLOCKS // 2 if halves else BLOCKS
    parts = []
    for own, came in ((own_a, in_a), (own_b, in_b)):
        own = own.at[0]
        merged, split = shares([load_logs(own, ROWS), load_logs(came, base)])
        if halves:
            lower = lax.broadcasted_iota(jnp.int32, merged.shape, 0) < blocks
            came_here = lower if came is in_a else jnp.logical_not(lower)
            merged = jnp.where(came_here, merged, load_logs(own, ROWS))
        store_logs(out_a if came is in_a else out_b, ROWS, merged)
        parts += split
    turned = columns(parts)
    for k, (own, came, out) in enumerate(((own_a, in_a, out_a), (own_b, in_b, out_b))):
        own = own.at[0]
        skip = blocks if (halves and k == 1) else 0
        for block in range(BLOCKS):
            rows = slice(block * BLOCK, (block + 1) * BLOCK)
            if skip <= block < skip + blocks:
                blend(
                    out,
                    turned,
                    2 * k,
                    block,
                    [(own, block * BLOCK), (came, (block - skip) * BLOCK)],
                )
            else:
                out[rows, :] = own[rows, :]


def finish_kernel(own, in_a, in_b, out):
    own = own.at[0]
    _, split = shares([load_logs(own, ROWS), load_logs(in_a, ROWS), load_logs(in_b, ROWS)])
    turned = columns(split)
    for block in range(BLOCKS):
        row = block * BLOCK
        blend(out, turned, 0, block, [(own, row), (in_a, row), (in_b, row)])


def whole(shape):
    return pl.BlockSpec(shape, lambda i: (0,) * len(shape))


def own_of(index):
    return pl.BlockSpec((1, MSG, COLS), lambda i: (index, 0, 0))


def params():
    return pltpu.CompilerParams(vmem_limit_bytes=VMEM_LIMIT)


def merge(own, index_a, index_b, in_a, in_b):
    halves = in_a.shape[0] != MSG
    message = jax.ShapeDtypeStruct((MSG, COLS), jnp.bfloat16)
    return pl.pallas_call(
        functools.partial(merge_kernel, halves),
        out_shape=(message, message),
        grid=(1,),
        in_specs=[own_of(index_a), own_of(index_b), whole(in_a.shape), whole(in_b.shape)],
        out_specs=(whole((MSG, COLS)), whole((MSG, COLS))),
        compiler_params=params(),
        cost_estimate=pl.CostEstimate(
            flops=8 * ROWS * COLS, transcendentals=0, bytes_accessed=12 * ROWS * COLS
        ),
        name="merge",
    )(own, own, in_a, in_b)


def finish(own, in_a, in_b):
    return pl.pallas_call(
        finish_kernel,
        out_shape=jax.ShapeDtypeStruct((ROWS, COLS), jnp.bfloat16),
        grid=(1,),
        in_specs=[own_of(len(SRC) - 1), whole((MSG, COLS)), whole((MSG, COLS))],
        out_specs=whole((ROWS, COLS)),
        compiler_params=params(),
        cost_estimate=pl.CostEstimate(
            flops=8 * ROWS * COLS, transcendentals=0, bytes_accessed=8 * ROWS * COLS
        ),
        name="finish",
    )(own, in_a, in_b)


def attend(piece, requests, query_parts, pair_parts):
    count, where, entry = requests
    anywhere = pl.BlockSpec(memory_space=pl.ANY)
    first = jnp.full((1,), piece * COLS, jnp.int32)
    smem = pl.BlockSpec(memory_space=pltpu.SMEM)
    n_in = len(query_parts) + len(pair_parts)

    def kernel(count_ref, where_ref, entry_ref, first_ref, *refs):
        attend_kernel(
            count_ref,
            where_ref,
            entry_ref,
            *refs[:n_in],
            [piece * COLS],
            *refs[n_in:],
        )

    return pl.pallas_call(
        kernel,
        out_shape=jax.ShapeDtypeStruct((len(SRC) + 1, MSG, COLS), jnp.bfloat16),
        in_specs=[smem] * 4 + [anywhere] * n_in,
        out_specs=pl.BlockSpec(memory_space=pltpu.VMEM),
        scratch_shapes=[
            pltpu.VMEM((len(SRC), ROWS, COLS), jnp.bfloat16),
            pltpu.VMEM((2, 128, NLEN, COLS), jnp.bfloat16),
            pltpu.VMEM((PLACES + 1, HEADS * BLOCK, 128), jnp.float32),
            pltpu.SemaphoreType.DMA((n_in,)),
        ],
        compiler_params=params(),
        cost_estimate=pl.CostEstimate(
            flops=MAXREQ * HEADS * 4 * BLOCK * NLEN * HD,
            transcendentals=MAXREQ * HEADS * BLOCK * NLEN,
            bytes_accessed=26 * 1024 * 1024,
        ),
        name="attend",
    )(count, where, entry, first, *query_parts, *pair_parts)


def project_kernel(turn_ref, *refs):
    lhs_refs, w_ref, out_ref, rows = refs[:8], refs[8], refs[9], refs[10]
    for dt in range(NT):
        at = lax.rem(turn_ref[0] + dt, NT) * (2 * COLS)
        for piece in range(2):
            rows[:, pl.ds(pl.multiple_of(at + piece * COLS, COLS), COLS)] = lhs_refs[
                piece * NT + dt
            ][...]
    out_ref[...] = jnp.dot(rows[...], w_ref[...], preferred_element_type=jnp.float32).astype(
        jnp.bfloat16
    )


def project(turn, lhs, weight):
    tile = 256
    depth, width = weight.shape
    return pl.pallas_call(
        project_kernel,
        out_shape=jax.ShapeDtypeStruct((ROWS, width), jnp.bfloat16),
        grid=(ROWS // tile,),
        in_specs=[pl.BlockSpec(memory_space=pltpu.SMEM)]
        + [pl.BlockSpec((tile, COLS), lambda i: (i, 0))] * 8
        + [pl.BlockSpec((depth, width), lambda i: (0, 0))],
        out_specs=pl.BlockSpec((tile, width), lambda i: (i, 0)),
        scratch_shapes=[pltpu.VMEM((tile, depth), jnp.bfloat16)],
        compiler_params=params(),
        cost_estimate=pl.CostEstimate(
            flops=2 * ROWS * depth * width,
            transcendentals=0,
            bytes_accessed=2 * (ROWS * depth + depth * width + ROWS * width),
        ),
        name="project",
    )(turn, *lhs, weight)


def request_list(nb_shard, nb_row):
    my_x, my_z, my_c = (lax.axis_index(a) for a in ("x", "z", "c"))
    table = jnp.stack([nb_shard, nb_row]).reshape(1, 2 * BLOCKS * NBR)
    tables = lax.all_to_all(
        jnp.broadcast_to(table, (NZ, 2 * BLOCKS * NBR)), "z", split_axis=0, concat_axis=0, tiled=True
    )
    order = (my_z + jnp.array(SRC, jnp.int32)) % NZ
    pick = (order[:, None] == jnp.arange(NZ, dtype=jnp.int32)[None, :]).astype(jnp.int32)
    tables = jnp.sum(pick[:, :, None] * tables[None], axis=1)
    shard = tables[:, : BLOCKS * NBR].reshape(-1)
    row = tables[:, BLOCKS * NBR :].reshape(-1)
    valid = (shard // NC) % NZ == my_z
    near = (shard // (NC * NZ) - my_x) % NX
    other = (shard % NC + my_c) % NC
    entry = (near * NC + other) * 16 + row
    where = jnp.arange(shard.shape[0], dtype=jnp.int32) // NBR
    seen = valid.astype(jnp.int32)
    ids = jnp.arange(shard.shape[0], dtype=jnp.int32)
    rank = jnp.sum(jnp.where(ids[None, :] < ids[:, None], seen[None, :], 0), axis=1)
    slot = jnp.arange(MAXREQ, dtype=jnp.int32)
    hit = valid[None, :] & (rank[None, :] == slot[:, None])
    where_list = jnp.sum(jnp.where(hit, where[None, :], 0), axis=1)
    where_list = jnp.where(slot < jnp.sum(seen), where_list, PLACES)
    entry_list = jnp.sum(jnp.where(hit, entry[None, :], 0), axis=1)
    return jnp.sum(seen).reshape(1), where_list, entry_list


def per_device(queries, db_keys, db_values, nb_shard, nb_row, out_weight):
    weight = lax.all_gather(out_weight, ("x", "z", "c"), axis=0, tiled=True)
    requests = request_list(nb_shard, nb_row)

    upcoming = seq_shift(queries[:BLOCK], 1)
    extended = jnp.concatenate([queries[BLOCK - 1 :], upcoming[: BLOCK - 1]], axis=0)

    up, down = [extended], [extended]
    for _ in range(3):
        up.append(shift(up[-1], "z", 1))
        down.append(shift(down[-1], "z", -1))
    far_low = shift(up[3][:HALF], "z", 1)
    far_high = shift(down[3][HALF:], "z", -1)
    query_parts = [far_low, far_high, up[3], down[3], up[2], down[2], up[1], down[1], extended]

    first_in = tuple(requests)
    gathered = []
    for piece in range(2):
        cols = slice(piece * COLS, (piece + 1) * COLS)
        own = jnp.stack([db_keys[:, :, cols], db_values[:, :, cols]])
        if piece:
            own = after(own, keys2, values2)
        ahead = shift(own, "x", 1)
        behind = shift(own, "x", -1)
        ahead, behind = lax.optimization_barrier((ahead, behind, *first_in))[:2]
        keys2 = shift(ahead[0], "x", 1)
        values2 = shift(behind[1], "x", -1)
        parts = []
        for part in (own, ahead, behind, keys2, values2):
            parts += [part, shift(part, "c", 1)]
        own = attend(piece, requests, query_parts, parts)
        first_in = (own,)
        far_logs = own[0, ROWS:]
        in_a = shift(jnp.concatenate([own[0, :HALF], far_logs], axis=0), "z", -1)
        in_b = shift(jnp.concatenate([own[0, HALF:ROWS], far_logs], axis=0), "z", 1)
        for step in range(3):
            out_a, out_b = merge(own, 1 + 2 * step, 2 + 2 * step, in_a, in_b)
            in_a = shift(out_a, "z", -1)
            in_b = shift(out_b, "z", 1)
            if step == 1 and not piece:
                requests = lax.optimization_barrier((*requests, out_a, out_b))[:3]
        attended = finish(own, in_a, in_b)
        tail = seq_shift(attended[ROWS - BLOCK :], -1)
        placed = jnp.concatenate([tail[1:], attended[: ROWS - (BLOCK - 1)]], axis=0)
        ahead = shift(placed, "tp", 1)
        behind = shift(placed, "tp", -1)
        low = shift(ahead[:HALF], "tp", 1)
        high = shift(behind[HALF:], "tp", -1)
        gathered += [placed, ahead, jnp.concatenate([low, high], axis=0), behind]
    turn = lax.axis_index("tp").astype(jnp.int32).reshape(1)
    return project(turn, gathered, weight)


def solution(mesh):
    grid = Mesh(mesh.devices.reshape(NX, NZ, NC, NT), ("x", "z", "c", "tp"))
    seq = ("x", "z", "c")
    placed = (
        P(seq, "tp"),
        P(seq, None, "tp"),
        P(seq, None, "tp"),
        P(seq, None),
        P(seq, None),
        P(seq, "tp"),
    )
    return jax.shard_map(
        per_device, mesh=grid, in_specs=placed, out_specs=P(seq, "tp"), check_vma=False
    )
```
